32 devices in a mesh: gx: 4 (over y, x), gy: 8 (over z, core).
Axes of the slice: x: 2, y: 2, z: 4, core: 2. Of those that a mesh axis runs over, the one named last changes fastest.
Arguments:
- fields: bfloat16 [8, 64, 128, 192], P(None, 'gx', 'gy'), may hold values from -6 to 6
- gain_window: float32 [192], replicated, may hold values from 0.1 to 1.9
- mixer_fine: bfloat16 [192, 576], replicated, may hold values from -3 to 3
- output_fine: bfloat16 [192, 192], replicated, may hold values from -0.4375 to 0.4375
- gain_hidden: float32 [192], replicated, may hold values from 0.1 to 1.9
- expand: bfloat16 [192, 768], replicated, may hold values from -0.4375 to 0.4375
- contract: bfloat16 [768, 192], replicated, may hold values from -0.21875 to 0.21875
- gain_merge: float32 [768], replicated, may hold values from 0.1 to 1.9
- merge_weight: bfloat16 [768, 384], replicated, may hold values from -0.21875 to 0.21875
- gain_coarse: float32 [384], replicated, may hold values from 0.1 to 1.9
- mixer_coarse: bfloat16 [384, 1152], replicated, may hold values from -2.1 to 2.1
- output_coarse: bfloat16 [384, 384], replicated, may hold values from -0.3125 to 0.3125
Outputs:
- merged: bfloat16 [8, 32, 64, 384], P(None, 'gx', 'gy')
- coarse: bfloat16 [8, 32, 64, 384], P(None, 'gx', 'gy')
The draws below stay inside these ranges and needn't reach their ends.
All inputs are finite; a program needn't handle non-finite values.
Results may differ from the reference program's by a relative error of at most 0.019.
Values may be sent and summed in bfloat16 or wider, within the bound.
A program may use at most 128 MiB of HBM per device.

```python
import math
import jax
import jax.numpy as jnp
from jax import lax

BATCH = 8
WIN = 16
C2 = 192
C3 = 384
HID2 = 768
HEADS2 = 6
HEADS3 = 12
H2 = 64
W2 = 128
H3 = 32
W3 = 64


def normal_block(key, rows_count, columns):
    return jax.random.truncated_normal(key, -5.0, 5.0, (rows_count, columns), jnp.float32) / math.sqrt(rows_count)


def draw_fields(key, part):
    key_base = jax.random.fold_in(key, 0)
    values = jax.random.truncated_normal(key_base, -6.0, 6.0, (BATCH, H2, W2, C2), jnp.float32)
    return values.astype(jnp.bfloat16)


def draw_mixer_fine(key, part):
    key_base = jax.random.fold_in(key, 0)
    base = normal_block(key_base, C2, 3 * C2)
    values = base
    return jnp.clip(values, -3.0, 3.0).astype(jnp.bfloat16)


def draw_mixer_coarse(key, part):
    key_base = jax.random.fold_in(jax.random.fold_in(key, 7), 0)
    base = normal_block(key_base, C3, 3 * C3)
    values = base
    return jnp.clip(values, -2.1, 2.1).astype(jnp.bfloat16)


def scatter_about(rng, shape, scale, bound, kind=jnp.bfloat16):
    return jnp.clip(scale * jax.random.normal(rng, shape, jnp.float32), -bound, bound).astype(kind)


def setup_inputs(seed: int = 0) -> dict:
    key_of = jax.random.split(jax.random.key(seed), 13)
    return {
        "fields": draw_fields(jax.random.fold_in(key_of[12], 71), 0),
        "gain_window": jnp.clip(1.0 + 0.18 * jax.random.normal(key_of[1], (C2,), jnp.float32), 0.1, 1.9),
        "mixer_fine": draw_mixer_fine(jax.random.fold_in(key_of[12], 71), 0),
        "output_fine": scatter_about(key_of[3], (C2, C2), C2 ** -0.5, 0.4375),
        "gain_hidden": jnp.clip(1.0 + 0.18 * jax.random.normal(key_of[4], (C2,), jnp.float32), 0.1, 1.9),
        "expand": scatter_about(key_of[5], (C2, HID2), C2 ** -0.5, 0.4375),
        "contract": scatter_about(key_of[6], (HID2, C2), HID2 ** -0.5, 0.21875),
        "gain_merge": jnp.clip(1.0 + 0.18 * jax.random.normal(key_of[7], (4 * C2,), jnp.float32), 0.1, 1.9),
        "merge_weight": scatter_about(key_of[8], (4 * C2, C3), (4 * C2) ** -0.5, 0.21875),
        "gain_coarse": jnp.clip(1.0 + 0.18 * jax.random.normal(key_of[9], (C3,), jnp.float32), 0.1, 1.9),
        "mixer_coarse": draw_mixer_coarse(jax.random.fold_in(key_of[12], 71), 0),
        "output_coarse": scatter_about(key_of[11], (C3, C3), C3 ** -0.5, 0.3125),
    }


epsilon = 1e-05

def normalize(values, scaling):
    values = values.astype(jnp.float32)
    center = values - lax.optimization_barrier(jnp.mean(values, -1, keepdims=True))
    spread = lax.optimization_barrier(jnp.mean(center * center, -1, keepdims=True))
    return center * lax.rsqrt(spread + epsilon) * scaling.astype(jnp.float32)

def attend(query_rows, key_rows, value_rows, head_count):
    windows, length, channels = query_rows.shape
    head_size = channels // head_count
    split_query = query_rows.astype(jnp.float32).reshape(windows, length, head_count, head_size)
    split_keys = key_rows.astype(jnp.float32).reshape(windows, -1, head_count, head_size)
    split_values = value_rows.astype(jnp.float32).reshape(windows, -1, head_count, head_size)
    scores = jnp.einsum('nqhd,nkhd->nhqk', split_query, split_keys) / math.sqrt(head_size)
    highest = lax.optimization_barrier(jnp.max(scores, -1, keepdims=True))
    powers = jnp.exp(scores - highest)
    attention = (powers / lax.optimization_barrier(jnp.sum(powers, -1, keepdims=True))).astype(jnp.bfloat16)
    context = jnp.einsum('nhqk,nkhd->nqhd', attention.astype(jnp.float32), split_values)
    return context.reshape(windows, length, channels).astype(jnp.bfloat16)

def attention_layer(tokens, scaling, mixer, output_weight, head_count):
    channels = tokens.shape[-1]
    normed = normalize(tokens, scaling).astype(jnp.bfloat16)
    projected = jnp.dot(normed, mixer, preferred_element_type=jnp.float32).astype(jnp.bfloat16)
    context = attend(projected[..., :channels], projected[..., channels:2 * channels], projected[..., 2 * channels:], head_count)
    update = jnp.dot(context, output_weight, preferred_element_type=jnp.float32)
    return (tokens.astype(jnp.float32) + update).astype(jnp.bfloat16)

def feed_forward(tokens, scaling, expand, contract):
    normed = normalize(tokens, scaling).astype(jnp.bfloat16)
    hidden = jax.nn.gelu(jnp.dot(normed, expand, preferred_element_type=jnp.float32), approximate=False).astype(jnp.bfloat16)
    return (tokens.astype(jnp.float32) + jnp.dot(hidden, contract, preferred_element_type=jnp.float32)).astype(jnp.bfloat16)

def merge_patches(tokens, scaling, merge_weight):
    samples, height, breadth, channels = tokens.shape
    patches = tokens.reshape(samples, height // 2, 2, breadth // 2, 2, channels).transpose(0, 1, 3, 4, 2, 5)
    patches = patches.reshape(samples, height // 2, breadth // 2, 4 * channels)
    normed = normalize(patches, scaling).astype(jnp.bfloat16)
    return jnp.dot(normed, merge_weight, preferred_element_type=jnp.float32).astype(jnp.bfloat16)

def to_windows(tokens, window):
    samples, height, breadth, channels = tokens.shape
    blocks = tokens.reshape(samples, height // window, window, breadth // window, window, channels)
    return blocks.transpose(0, 1, 3, 2, 4, 5).reshape(samples * (height // window), breadth // window, window * window, channels)

def from_windows(blocks, samples, height, breadth, window):
    channels = blocks.shape[-1]
    tokens = blocks.reshape(samples, height // window, breadth // window, window, window, channels)
    return tokens.transpose(0, 1, 3, 2, 4, 5).reshape(samples, height, breadth, channels)

def reference(fields, gain_window, mixer_fine, output_fine, gain_hidden, expand, contract, gain_merge, merge_weight, gain_coarse, mixer_coarse, output_coarse):
    offset = WIN // 2
    rolled = jnp.roll(fields, (-offset, -offset), axis=(1, 2))

    def fine_block(blocks):
        attended = attention_layer(blocks, gain_window, mixer_fine, output_fine, HEADS2)
        return feed_forward(attended, gain_hidden, expand, contract)
    refined = lax.map(fine_block, to_windows(rolled, WIN))
    refined = jnp.roll(from_windows(refined, BATCH, H2, W2, WIN), (offset, offset), axis=(1, 2))
    merged = lax.map(lambda sample: merge_patches(sample[None], gain_merge, merge_weight)[0], refined)

    def coarse_block(blocks):
        return attention_layer(blocks, gain_coarse, mixer_coarse, output_coarse, HEADS3)
    coarse = from_windows(lax.map(coarse_block, to_windows(merged, WIN)), BATCH, H3, W3, WIN)
    return (merged, coarse)
```

```python
import functools
import math

import jax
import jax.numpy as jnp
from jax import lax
from jax.experimental import pallas as pl
from jax.experimental.pallas import tpu as pltpu
from jax.sharding import PartitionSpec as P

HEAD = 32
LANES = 128
EPSILON = 1e-05
F32 = jnp.float32
BF16 = jnp.bfloat16
MESH = pl.DeviceIdType.MESH


def dot(a, b):
    return jnp.dot(a, b, preferred_element_type=F32)


def normalize(values, gain):
    center = values - jnp.mean(values, -1, keepdims=True)
    spread = jnp.mean(center * center, -1, keepdims=True)
    return (center * lax.rsqrt(spread + EPSILON) * gain).astype(BF16)


def gelu(x):
    return 0.5 * x * (1.0 + lax.erf(x * (1.0 / math.sqrt(2.0))))


def attention(queries, keys, values):
    channels = queries.shape[-1]
    factor = math.log2(math.e) / math.sqrt(HEAD)
    groups = []
    for low in range(0, channels, LANES):
        width = min(LANES, channels - low)
        q, k, v = (t[:, low : low + width] for t in (queries, keys, values))
        owner = lax.broadcasted_iota(jnp.int32, (1, width), 1) // HEAD
        context = None
        for head in range(width // HEAD):
            mine = owner == head
            scores = lax.dot_general(
                q * mine.astype(F32).astype(BF16), k, (((1,), (1,)), ((), ())),
                preferred_element_type=F32,
            )
            highest = jnp.max(scores, -1, keepdims=True)
            powers = jnp.exp2((scores - highest) * factor)
            total = jnp.sum(powers, -1, keepdims=True)
            part = dot(powers.astype(BF16), v) * (1.0 / total)
            context = part if context is None else jnp.where(mine, part, context)
        groups.append(context.astype(BF16))
    return groups


def project(groups, weight_ref):
    total = None
    for index, group in enumerate(groups):
        part = dot(group, weight_ref[index * LANES : index * LANES + group.shape[-1], :])
        total = part if total is None else total + part
    return total


def kernel(
    nx, ny,
    fields, gain_window, mixer_fine, output_fine, gain_hidden, expand, contract,
    gain_merge, merge_weight, gain_coarse, mixer_coarse, output_coarse,
    merged_out, coarse_out,
    fbuf, mbuf, mhome, cbuf, obuf, wsplit, perm_fine, perm_coarse,
    f_send, f_recv, m_send, m_recv, c_send, c_recv, o_send, o_recv,
):
    samples, _, half, _, channels = fbuf.shape
    side = 2 * half
    tokens = side * side
    quarter = half // 2
    piece = quarter * quarter
    patch = 4 * piece
    wide = merged_out.shape[-1]
    x = lax.axis_index("gx")
    y = lax.axis_index("gy")

    def at(dx, dy):
        return (lax.rem(x + dx + nx, nx), lax.rem(y + dy + ny, ny))

    def field_copy(n, a, b):
        slot = (1 - a) * 2 + (1 - b)
        source = fields.at[n, pl.ds(a * half, half), b]
        target = fbuf.at[n, slot]
        if a == 1 and b == 1:
            return pltpu.make_async_copy(source, target, f_recv.at[n])
        return pltpu.make_async_remote_copy(
            source, target, f_send.at[n, slot], f_recv.at[n],
            device_id=at(a - 1, b - 1), device_id_type=MESH,
        )

    ORDER = ((0, 0), (0, 1), (1, 0), (1, 1))

    barrier = pltpu.get_barrier_semaphore()
    reach = [(dx, dy) for dx in range(-2, 3) for dy in range(-2, 3) if (dx, dy) != (0, 0)]
    for dx, dy in reach:
        pl.semaphore_signal(barrier, inc=1, device_id=at(dx, dy), device_id_type=MESH)
    pl.semaphore_wait(barrier, len(reach))

    def start_fields(n, carry):
        for a, b in ORDER:
            field_copy(n, a, b).start()
        return carry

    lax.fori_loop(0, samples, start_fields, 0)

    for index in range(3):
        wsplit[index] = mixer_fine[:, index * channels : (index + 1) * channels]
    row = lax.broadcasted_iota(jnp.int32, (tokens, tokens), 0)
    col = lax.broadcasted_iota(jnp.int32, (tokens, tokens), 1)
    parity, rest = row // patch, row % patch
    quadrant, within = rest // piece, rest % piece
    origin = (
        quadrant * (half * half)
        + (2 * (within // quarter) + parity % 2) * half
        + 2 * (within % quarter)
        + parity // 2
    )
    perm_fine[...] = (origin == col).astype(F32).astype(BF16)
    row = lax.broadcasted_iota(jnp.int32, (patch, patch), 0)
    col = lax.broadcasted_iota(jnp.int32, (patch, patch), 1)
    down, across = row // half, row % half
    origin = (
        (down // quarter * 2 + across // quarter) * piece
        + (down % quarter) * quarter
        + across % quarter
    )
    perm_coarse[...] = (origin == col).astype(F32).astype(BF16)

    def home_copy(n, a, b):
        source = mbuf.at[n, a * 2 + b]
        target = mhome.at[n, (1 - a) * 2 + (1 - b)]
        if a == 0 and b == 0:
            return pltpu.make_async_copy(source, target, m_recv)
        return pltpu.make_async_remote_copy(
            source, target, m_send.at[n, a * 2 + b], m_recv,
            device_id=at(a, b), device_id_type=MESH,
        )

    def owner_copy(n, a, b):
        hx, hy = at(a, b)
        member = n % 4
        ox = hx - hx % 2 + member // 2
        oy = hy - hy % 2 + member % 2
        source = mbuf.at[n, a * 2 + b]
        target = cbuf.at[n // 4, (hx % 2) * 2 + hy % 2, (1 - a) * 2 + (1 - b)]
        here = jnp.logical_and(ox == x, oy == y)
        local = pltpu.make_async_copy(source, target, c_recv.at[n // 4])
        remote = pltpu.make_async_remote_copy(
            source, target, c_send.at[n, a * 2 + b], c_recv.at[n // 4],
            device_id=(ox, oy), device_id_type=MESH,
        )
        return here, local, remote

    def fine(n, carry):
        pltpu.make_async_copy(fbuf.at[n], fbuf.at[n], f_recv.at[n]).wait()
        window = fbuf[n].astype(F32).reshape(tokens, channels).astype(BF16)
        value = dot(perm_fine[...], window)
        normed = normalize(value, gain_window[...])
        q, k, v = (dot(normed, wsplit[index]).astype(BF16) for index in range(3))
        attended = (value + project(attention(q, k, v), output_fine)).astype(BF16).astype(F32)
        normed = normalize(attended, gain_hidden[...])
        hidden = gelu(dot(normed, expand[...])).astype(BF16)
        refined = (attended + dot(hidden, contract[...])).astype(BF16).astype(F32)
        slabs = [refined[p * patch : (p + 1) * patch] for p in range(4)]
        mean = sum(jnp.sum(s, -1, keepdims=True) for s in slabs) * (1.0 / (4 * channels))
        slabs = [s - mean for s in slabs]
        spread = sum(jnp.sum(s * s, -1, keepdims=True) for s in slabs) * (1.0 / (4 * channels))
        scale = lax.rsqrt(spread + EPSILON)
        merged = None
        for p, s in enumerate(slabs):
            gain = gain_merge[:, p * channels : (p + 1) * channels]
            part = dot(
                (s * scale * gain).astype(BF16), merge_weight[p * channels : (p + 1) * channels, :]
            )
            merged = part if merged is None else merged + part
        mbuf[n] = merged.astype(BF16).reshape(4, piece, wide)
        for a, b in ORDER:
            here, local, remote = owner_copy(n, a, b)
            pl.when(here)(local.start)
            pl.when(jnp.logical_not(here))(remote.start)
        for a, b in ORDER:
            home_copy(n, a, b).start()
        return carry

    lax.fori_loop(0, samples, fine, 0)

    bx, by = x - x % 2, y - y % 2
    me = (x % 2) * 2 + y % 2

    def result_copy(s, home):
        hx, hy = bx + home // 2, by + home % 2
        n = s * 4 + me
        local = pltpu.make_async_copy(obuf.at[s, home], coarse_out.at[n], o_recv)
        remote = pltpu.make_async_remote_copy(
            obuf.at[s, home], coarse_out.at[n], o_send.at[s, home], o_recv,
            device_id=(hx, hy), device_id_type=MESH,
        )
        return home == me, local, remote

    def coarse(s, carry):
        pltpu.make_async_copy(cbuf.at[s], cbuf.at[s], c_recv.at[s]).wait()
        merged = cbuf[s].reshape(4 * patch, wide).astype(F32)
        normed = normalize(merged, gain_coarse[...])
        q, k, v = (
            dot(normed, mixer_coarse[:, index * wide : (index + 1) * wide]).astype(BF16)
            for index in range(3)
        )
        out = (merged + project(attention(q, k, v), output_coarse)).astype(BF16)
        for home in range(4):
            obuf[s, home] = dot(
                perm_coarse[...], out[home * patch : (home + 1) * patch]
            ).astype(BF16)
            here, local, remote = result_copy(s, home)
            pl.when(here)(local.start)
            pl.when(jnp.logical_not(here))(remote.start)
        return carry

    lax.fori_loop(0, samples // 4, coarse, 0)

    pltpu.make_async_copy(mhome, mhome, m_recv).wait()

    def settle(n, carry):
        merged_out[n] = dot(perm_coarse[...], mhome[n].reshape(patch, wide)).astype(BF16)
        for a, b in ORDER:
            if (a, b) != (1, 1):
                field_copy(n, a, b).wait_send()
            if (a, b) != (0, 0):
                home_copy(n, a, b).wait_send()
            here, _, remote = owner_copy(n, a, b)
            pl.when(jnp.logical_not(here))(remote.wait_send)
        return carry

    lax.fori_loop(0, samples, settle, 0)
    for s in range(samples // 4):
        for home in range(4):
            here, _, remote = result_copy(s, home)
            pl.when(jnp.logical_not(here))(remote.wait_send)
    pltpu.make_async_copy(coarse_out, coarse_out, o_recv).wait()


def shards(nx, ny, fields, *weights):
    samples, side, _, channels = fields.shape
    half = side // 2
    wide = weights[7].shape[-1]
    piece = half * half // 4
    weights = [w.reshape(1, -1) if w.ndim == 1 else w for w in weights]
    shape = jax.ShapeDtypeStruct((samples, 4 * piece, wide), BF16)
    vmem = pl.BlockSpec(memory_space=pltpu.VMEM)
    hbm = pl.BlockSpec(memory_space=pl.ANY)
    dma = pltpu.SemaphoreType.DMA
    merged, coarse = pl.pallas_call(
        functools.partial(kernel, nx, ny),
        out_shape=(shape, shape),
        in_specs=[hbm] + [vmem] * len(weights),
        out_specs=(vmem, hbm),
        scratch_shapes=[
            pltpu.VMEM((samples, 4, half, half, channels), BF16),
            pltpu.VMEM((samples, 4, piece, wide), BF16),
            pltpu.VMEM((samples, 4, piece, wide), BF16),
            pltpu.VMEM((samples // 4, 4, 4, piece, wide), BF16),
            pltpu.VMEM((samples // 4, 4, 4 * piece, wide), BF16),
            pltpu.VMEM((3, channels, channels), BF16),
            pltpu.VMEM((side * side, side * side), BF16),
            pltpu.VMEM((4 * piece, 4 * piece), BF16),
            dma((samples, 4)), dma((samples,)),
            dma((samples, 4)), dma,
            dma((samples, 4)), dma((samples // 4,)),
            dma((samples // 4, 4)), dma,
        ],
        compiler_params=pltpu.CompilerParams(
            collective_id=0, has_side_effects=True, vmem_limit_bytes=48 * 1024 * 1024
        ),
        name="encoder",
    )(fields.reshape(samples, side, 2, half, channels), *weights)
    return tuple(t.reshape(samples, half, half, wide) for t in (merged, coarse))


def solution(mesh):
    in_specs = (P(None, "gx", "gy", None),) + (P(),) * 11
    out_specs = (P(None, "gx", "gy", None), P(None, "gx", "gy", None))
    body = functools.partial(shards, mesh.shape["gx"], mesh.shape["gy"])
    return jax.shard_map(body, mesh=mesh, in_specs=in_specs, out_specs=out_specs, check_vma=False)
```

```python
import functools
import math

import jax
import jax.numpy as jnp
from jax import lax
from jax.experimental import pallas as pl
from jax.experimental.pallas import tpu as pltpu
from jax.sharding import PartitionSpec as P

HEAD = 32
LANES = 128
EPSILON = 1e-05
F32 = jnp.float32
BF16 = jnp.bfloat16
MESH = pl.DeviceIdType.MESH


def dot(a, b):
    return jnp.dot(a, b, preferred_element_type=F32)


def dot_nt(a, b):
    return lax.dot_general(a, b, (((1,), (1,)), ((), ())), preferred_element_type=F32)


def normalize(values, gain):
    center = values - jnp.mean(values, -1, keepdims=True)
    spread = jnp.mean(center * center, -1, keepdims=True)
    return (center * lax.rsqrt(spread + EPSILON) * gain).astype(BF16)


def gelu(x):
    return 0.5 * x * (1.0 + lax.erf(x * (1.0 / math.sqrt(2.0))))


def attention(queries, keys, values):
    channels = queries.shape[-1]
    factor = math.log2(math.e) / math.sqrt(HEAD)
    groups = []
    for low in range(0, channels, LANES):
        width = min(LANES, channels - low)
        q, k, v = (t[:, low : low + width] for t in (queries, keys, values))
        owner = lax.broadcasted_iota(jnp.int32, (1, width), 1) // HEAD
        context = None
        for head in range(width // HEAD):
            mine = owner == head
            scores = dot_nt(q * mine.astype(F32).astype(BF16), k)
            highest = jnp.max(scores, -1, keepdims=True)
            powers = jnp.exp2((scores - highest) * factor)
            total = jnp.sum(powers, -1, keepdims=True)
            part = dot(powers.astype(BF16), v) * (1.0 / total)
            context = part if context is None else jnp.where(mine, part, context)
        groups.append(context.astype(BF16))
    return groups


def project(groups, weight_ref):
    total = None
    for index, group in enumerate(groups):
        part = dot(group, weight_ref[index * LANES : index * LANES + group.shape[-1], :])
        total = part if total is None else total + part
    return total


def kernel(
    nx, ny,
    fields, *refs
):
    count = (len(refs) - 16) // 2
    weights_hbm, (mhome, coarse_out) = refs[:count], refs[count : count + 2]
    weights = refs[count + 2 : 2 * count + 2]
    (
        gain_window, mixer_fine, output_fine, gain_hidden, expand, contract,
        gain_merge, merge_weight, gain_coarse, mixer_coarse, output_coarse,
    ) = weights
    (
    fbuf, mbuf, cbuf, obuf, wsplit, perm_fine,
    f_send, f_recv, m_send, m_recv, c_send, c_recv, o_send, o_recv,
    w_recv,
    ) = refs[2 * count + 2 :]
    samples, _, half, _, channels = fbuf.shape
    side = 2 * half
    tokens = side * side
    quarter = half // 2
    piece = quarter * quarter
    patch = 4 * piece
    wide = mhome.shape[-1]
    x = lax.axis_index("gx")
    y = lax.axis_index("gy")

    def at(dx, dy):
        return (lax.rem(x + dx + nx, nx), lax.rem(y + dy + ny, ny))

    reach = [(dx, dy) for dx in (-1, 0, 1) for dy in (-1, 0, 1) if (dx, dy) != (0, 0)]
    barrier = pltpu.get_barrier_semaphore()
    for dx, dy in reach:
        pl.semaphore_signal(barrier, inc=1, device_id=at(dx, dy), device_id_type=MESH)
    loads = [
        pltpu.make_async_copy(source, target, w_recv.at[index])
        for index, (source, target) in enumerate(zip(weights_hbm, weights))
    ]
    for load in loads:
        load.start()
    def field_copy(n, a, b):
        slot = (1 - a) * 2 + (1 - b)
        source = fields.at[n, pl.ds(a * half, half), b]
        target = fbuf.at[n, slot]
        if a == 1 and b == 1:
            return pltpu.make_async_copy(source, target, f_recv.at[n])
        return pltpu.make_async_remote_copy(
            source, target, f_send.at[n, slot], f_recv.at[n],
            device_id=at(a - 1, b - 1), device_id_type=MESH,
        )

    ORDER = ((0, 0), (0, 1), (1, 0), (1, 1))

    pl.semaphore_wait(barrier, len(reach))

    def start_fields(n, carry):
        for a, b in ORDER:
            field_copy(n, a, b).start()
        return carry

    ahead = min(3, samples)
    lax.fori_loop(0, ahead, start_fields, 0)

    for load in loads[:8]:
        load.wait()
    for index in range(3):
        wsplit[index] = mixer_fine[:, index * channels : (index + 1) * channels]
    row = lax.broadcasted_iota(jnp.int32, (tokens, tokens), 0)
    col = lax.broadcasted_iota(jnp.int32, (tokens, tokens), 1)
    parity, rest = row // patch, row % patch
    quadrant, within = rest // piece, rest % piece
    origin = (
        quadrant * (half * half)
        + (2 * (within // quarter) + parity % 2) * half
        + 2 * (within % quarter)
        + parity // 2
    )
    perm_fine[...] = (origin == col).astype(F32).astype(BF16)
    def home_copy(n, a, b):
        source = mbuf.at[n, a * 2 + b]
        target = mhome.at[n, (1 - a) * 2 + (1 - b)]
        if a == 0 and b == 0:
            return pltpu.make_async_copy(source, target, m_recv)
        return pltpu.make_async_remote_copy(
            source, target, m_send.at[n, a * 2 + b], m_recv,
            device_id=at(a, b), device_id_type=MESH,
        )

    def owner_copy(n, a, b):
        hx, hy = at(a, b)
        member = n % 4
        ox = hx - hx % 2 + member // 2
        oy = hy - hy % 2 + member % 2
        source = mbuf.at[n, a * 2 + b]
        target = cbuf.at[n // 4, (hx % 2) * 2 + hy % 2, (1 - a) * 2 + (1 - b)]
        here = jnp.logical_and(ox == x, oy == y)
        local = pltpu.make_async_copy(source, target, c_recv.at[n // 4])
        remote = pltpu.make_async_remote_copy(
            source, target, c_send.at[n, a * 2 + b], c_recv.at[n // 4],
            device_id=(ox, oy), device_id_type=MESH,
        )
        return here, local, remote

    def fine(n, carry):
        @pl.when(n + ahead < samples)
        def _():
            start_fields(n + ahead, 0)

        pltpu.make_async_copy(fbuf.at[n], fbuf.at[n], f_recv.at[n]).wait()
        window = fbuf[n].astype(F32).reshape(tokens, channels).astype(BF16)
        value = dot(perm_fine[...], window)
        normed = normalize(value, gain_window[...][None])
        q, k, v = (dot(normed, wsplit[index]).astype(BF16) for index in range(3))
        attended = (value + project(attention(q, k, v), output_fine)).astype(BF16).astype(F32)
        normed = normalize(attended, gain_hidden[...][None])
        hidden = gelu(dot(normed, expand[...])).astype(BF16)
        refined = (attended + dot_nt(hidden, contract[...])).astype(BF16).astype(F32)
        slabs = [refined[p * patch : (p + 1) * patch] for p in range(4)]
        mean = sum(jnp.sum(s, -1, keepdims=True) for s in slabs) * (1.0 / (4 * channels))
        slabs = [s - mean for s in slabs]
        spread = sum(jnp.sum(s * s, -1, keepdims=True) for s in slabs) * (1.0 / (4 * channels))
        scale = lax.rsqrt(spread + EPSILON)
        merged = None
        for p, s in enumerate(slabs):
            gain = gain_merge[...][None, p * channels : (p + 1) * channels]
            part = dot(
                (s * scale * gain).astype(BF16), merge_weight[p * channels : (p + 1) * channels, :]
            )
            merged = part if merged is None else merged + part
        mbuf[n] = merged.astype(BF16).reshape(4, piece, wide)
        for a, b in ORDER:
            here, local, remote = owner_copy(n, a, b)
            pl.when(here)(local.start)
            pl.when(jnp.logical_not(here))(remote.start)
        for a, b in ORDER:
            home_copy(n, a, b).start()
        return carry

    lax.fori_loop(0, samples, fine, 0)

    bx, by = x - x % 2, y - y % 2
    me = (x % 2) * 2 + y % 2

    def result_copy(s, home):
        hx, hy = bx + home // 2, by + home % 2
        n = s * 4 + me
        local = pltpu.make_async_copy(obuf.at[s, home], coarse_out.at[n], o_recv)
        remote = pltpu.make_async_remote_copy(
            obuf.at[s, home], coarse_out.at[n], o_send.at[s, home], o_recv,
            device_id=(hx, hy), device_id_type=MESH,
        )
        return home == me, local, remote

    def coarse(s, carry):
        pltpu.make_async_copy(cbuf.at[s], cbuf.at[s], c_recv.at[s]).wait()
        merged = cbuf[s].reshape(4 * patch, wide).astype(F32)
        normed = normalize(merged, gain_coarse[...][None])
        q, k, v = (
            dot(normed, mixer_coarse[:, index * wide : (index + 1) * wide]).astype(BF16)
            for index in range(3)
        )
        out = (merged + project(attention(q, k, v), output_coarse)).astype(BF16)
        for home in range(4):
            obuf[s, home] = out[home * patch : (home + 1) * patch]
            here, local, remote = result_copy(s, home)
            pl.when(here)(local.start)
            pl.when(jnp.logical_not(here))(remote.start)
        return carry

    for load in loads[8:]:
        load.wait()
    lax.fori_loop(0, samples // 4, coarse, 0)

    pltpu.make_async_copy(mhome, mhome, m_recv).wait()

    def settle(n, carry):
        for a, b in ORDER:
            if (a, b) != (1, 1):
                field_copy(n, a, b).wait_send()
            if (a, b) != (0, 0):
                home_copy(n, a, b).wait_send()
            here, _, remote = owner_copy(n, a, b)
            pl.when(jnp.logical_not(here))(remote.wait_send)
        return carry

    lax.fori_loop(0, samples, settle, 0)
    for s in range(samples // 4):
        for home in range(4):
            here, _, remote = result_copy(s, home)
            pl.when(jnp.logical_not(here))(remote.wait_send)
    pltpu.make_async_copy(coarse_out, coarse_out, o_recv).wait()


def natural_order(half, merged, coarse, merged_out, coarse_out):
    quarter = half // 2
    piece = quarter * quarter
    patch = 4 * piece
    row = lax.broadcasted_iota(jnp.int32, (patch, patch), 0)
    col = lax.broadcasted_iota(jnp.int32, (patch, patch), 1)
    down, across = row // half, row % half
    origin = (
        (down // quarter * 2 + across // quarter) * piece
        + (down % quarter) * quarter
        + across % quarter
    )
    order = (origin == col).astype(F32).astype(BF16)
    for n in range(merged.shape[0]):
        merged_out[n] = dot(order, merged[n]).astype(BF16)
        coarse_out[n] = dot(order, coarse[n]).astype(BF16)


def shards(nx, ny, fields, *weights):
    samples, side, _, channels = fields.shape
    half = side // 2
    wide = weights[7].shape[-1]
    piece = half * half // 4
    weights = [*weights[:5], weights[5].T, *weights[6:]]
    pieces = jax.ShapeDtypeStruct((samples, 4, piece, wide), BF16)
    shape = jax.ShapeDtypeStruct((samples, 4 * piece, wide), BF16)
    hbm = pl.BlockSpec(memory_space=pl.ANY)
    dma = pltpu.SemaphoreType.DMA
    merged, coarse = pl.pallas_call(
        functools.partial(kernel, nx, ny),
        out_shape=(pieces, shape),
        in_specs=[hbm] * (1 + len(weights)),
        out_specs=(hbm, hbm),
        scratch_shapes=[pltpu.VMEM(w.shape, w.dtype) for w in weights] + [
            pltpu.VMEM((samples, 4, half, half, channels), BF16),
            pltpu.VMEM((samples, 4, piece, wide), BF16),
            pltpu.VMEM((samples // 4, 4, 4, piece, wide), BF16),
            pltpu.VMEM((samples // 4, 4, 4 * piece, wide), BF16),
            pltpu.VMEM((3, channels, channels), BF16),
            pltpu.VMEM((side * side, side * side), BF16),
            dma((samples, 4)), dma((samples,)),
            dma((samples, 4)), dma,
            dma((samples, 4)), dma((samples // 4,)),
            dma((samples // 4, 4)), dma,
            dma((len(weights),)),
        ],
        compiler_params=pltpu.CompilerParams(
            collective_id=0, has_side_effects=True, vmem_limit_bytes=62 * 1024 * 1024
        ),
        name="encoder",
    )(fields.reshape(samples, side, 2, half, channels), *weights)
    steps = 2
    block = pl.BlockSpec((samples // steps, 4 * piece, wide), lambda step: (step, 0, 0))
    merged, coarse = pl.pallas_call(
        functools.partial(natural_order, half),
        grid=(steps,),
        out_shape=(shape, shape),
        in_specs=[block] * 2,
        out_specs=(block, block),
        name="natural_order",
    )(merged.reshape(shape.shape), coarse)
    return tuple(t.reshape(samples, half, half, wide) for t in (merged, coarse))


def solution(mesh):
    in_specs = (P(None, "gx", "gy", None),) + (P(),) * 11
    out_specs = (P(None, "gx", "gy", None), P(None, "gx", "gy", None))
    body = functools.partial(shards, mesh.shape["gx"], mesh.shape["gy"])
    return jax.shard_map(body, mesh=mesh, in_specs=in_specs, out_specs=out_specs, check_vma=False)
```

```python
import functools
import math

import jax
import jax.numpy as jnp
from jax import lax
from jax.experimental import pallas as pl
from jax.experimental.pallas import tpu as pltpu
from jax.sharding import PartitionSpec as P

HEAD = 32
LANES = 128
EPSILON = 1e-05
F32 = jnp.float32
BF16 = jnp.bfloat16
MESH = pl.DeviceIdType.MESH


def dot(a, b):
    return jnp.dot(a, b, preferred_element_type=F32)


def dot_nt(a, b):
    return lax.dot_general(a, b, (((1,), (1,)), ((), ())), preferred_element_type=F32)


def normalize(values, gain):
    center = values - jnp.mean(values, -1, keepdims=True)
    spread = jnp.mean(center * center, -1, keepdims=True)
    return (center * lax.rsqrt(spread + EPSILON) * gain).astype(BF16)


def gelu(x):
    return 0.5 * x * (1.0 + lax.erf(x * (1.0 / math.sqrt(2.0))))


def attention(queries, keys, values):
    channels = queries.shape[-1]
    factor = math.log2(math.e) / math.sqrt(HEAD)
    groups = []
    for low in range(0, channels, LANES):
        width = min(LANES, channels - low)
        q, k, v = (t[:, low : low + width] for t in (queries, keys, values))
        owner = lax.broadcasted_iota(jnp.int32, (1, width), 1) // HEAD
        context = None
        for head in range(width // HEAD):
            mine = owner == head
            scores = dot_nt(q * mine.astype(F32).astype(BF16), k)
            highest = jnp.max(scores, -1, keepdims=True)
            powers = jnp.exp2((scores - highest) * factor)
            total = jnp.sum(powers, -1, keepdims=True)
            part = dot(powers.astype(BF16), v) * (1.0 / total)
            context = part if context is None else jnp.where(mine, part, context)
        groups.append(context.astype(BF16))
    return groups


def project(groups, weight_ref):
    total = None
    for index, group in enumerate(groups):
        part = dot(group, weight_ref[index * LANES : index * LANES + group.shape[-1], :])
        total = part if total is None else total + part
    return total


def kernel(
    nx, ny,
    fields, *refs
):
    count = (len(refs) - 16) // 2
    weights_hbm, (mhome, coarse_out) = refs[:count], refs[count : count + 2]
    weights = refs[count + 2 : 2 * count + 2]
    (
        gain_window, mixer_fine, output_fine, gain_hidden, expand, contract,
        gain_merge, merge_weight, gain_coarse, mixer_coarse, output_coarse,
    ) = weights
    (
    fbuf, mbuf, cbuf, obuf, wsplit, perm_fine,
    f_send, f_recv, m_send, m_recv, c_send, c_recv, o_send, o_recv,
    w_recv,
    ) = refs[2 * count + 2 :]
    samples, _, half, _, channels = fbuf.shape
    side = 2 * half
    tokens = side * side
    quarter = half // 2
    piece = quarter * quarter
    patch = 4 * piece
    wide = mhome.shape[-1]
    x = lax.axis_index("gx")
    y = lax.axis_index("gy")

    def at(dx, dy):
        return (lax.rem(x + dx + nx, nx), lax.rem(y + dy + ny, ny))

    reach = [(dx, dy) for dx in (-1, 0, 1) for dy in (-1, 0, 1) if (dx, dy) != (0, 0)]
    barrier = pltpu.get_barrier_semaphore()
    for dx, dy in reach:
        pl.semaphore_signal(barrier, inc=1, device_id=at(dx, dy), device_id_type=MESH)
    loads = [
        pltpu.make_async_copy(source, target, w_recv.at[index])
        for index, (source, target) in enumerate(zip(weights_hbm, weights))
    ]
    for load in loads:
        load.start()
    def field_copy(n, a, b):
        slot = (1 - a) * 2 + (1 - b)
        source = fields.at[n, pl.ds(a * half, half), b]
        target = fbuf.at[n, slot]
        if a == 1 and b == 1:
            return pltpu.make_async_copy(source, target, f_recv.at[n])
        return pltpu.make_async_remote_copy(
            source, target, f_send.at[n, slot], f_recv.at[n],
            device_id=at(a - 1, b - 1), device_id_type=MESH,
        )

    ORDER = ((0, 0), (0, 1), (1, 0), (1, 1))

    pl.semaphore_wait(barrier, len(reach))

    def start_fields(n, carry):
        for a, b in ORDER:
            field_copy(n, a, b).start()
        return carry

    ahead = min(4, samples)
    lax.fori_loop(0, ahead, start_fields, 0)

    for load in loads[:8]:
        load.wait()
    for index in range(3):
        wsplit[index] = mixer_fine[:, index * channels : (index + 1) * channels]
    row = lax.broadcasted_iota(jnp.int32, (tokens, tokens), 0)
    col = lax.broadcasted_iota(jnp.int32, (tokens, tokens), 1)
    parity, rest = row // patch, row % patch
    quadrant, within = rest // piece, rest % piece
    origin = (
        quadrant * (half * half)
        + (2 * (within // quarter) + parity % 2) * half
        + 2 * (within % quarter)
        + parity // 2
    )
    perm_fine[...] = (origin == col).astype(F32).astype(BF16)
    def home_copy(n, a, b):
        source = mbuf.at[n, a * 2 + b]
        target = mhome.at[n, (1 - a) * 2 + (1 - b)]
        if a == 0 and b == 0:
            return pltpu.make_async_copy(source, target, m_recv)
        return pltpu.make_async_remote_copy(
            source, target, m_send.at[n, a * 2 + b], m_recv,
            device_id=at(a, b), device_id_type=MESH,
        )

    def owner_copy(n, a, b):
        hx, hy = at(a, b)
        member = n % 4
        ox = hx - hx % 2 + member // 2
        oy = hy - hy % 2 + member % 2
        source = mbuf.at[n, a * 2 + b]
        target = cbuf.at[n // 4, (hx % 2) * 2 + hy % 2, (1 - a) * 2 + (1 - b)]
        here = jnp.logical_and(ox == x, oy == y)
        local = pltpu.make_async_copy(source, target, c_recv.at[n // 4])
        remote = pltpu.make_async_remote_copy(
            source, target, c_send.at[n, a * 2 + b], c_recv.at[n // 4],
            device_id=(ox, oy), device_id_type=MESH,
        )
        return here, local, remote

    group = 2

    def fine(step, carry):
        first = step * group

        for w in range(group):
            @pl.when(first + w + ahead < samples)
            def _():
                start_fields(first + w + ahead, 0)

        values = []
        for w in range(group):
            n = first + w
            pltpu.make_async_copy(fbuf.at[n], fbuf.at[n], f_recv.at[n]).wait()
            window = fbuf[n].astype(F32).reshape(tokens, channels).astype(BF16)
            values.append(dot(perm_fine[...], window))
        value = jnp.concatenate(values, axis=0)
        normed = normalize(value, gain_window[...][None])
        q, k, v = (dot(normed, wsplit[index]).astype(BF16) for index in range(3))
        parts = [
            attention(*(t[w * tokens : (w + 1) * tokens] for t in (q, k, v)))
            for w in range(group)
        ]
        context = [jnp.concatenate(c, axis=0) for c in zip(*parts)]
        attended = (value + project(context, output_fine)).astype(BF16).astype(F32)
        normed = normalize(attended, gain_hidden[...][None])
        hidden = gelu(dot(normed, expand[...])).astype(BF16)
        refined = (attended + dot_nt(hidden, contract[...])).astype(BF16).astype(F32)
        slabs = [
            jnp.concatenate(
                [refined[w * tokens + p * patch : w * tokens + (p + 1) * patch] for w in range(group)],
                axis=0,
            )
            for p in range(4)
        ]
        mean = sum(jnp.sum(s, -1, keepdims=True) for s in slabs) * (1.0 / (4 * channels))
        slabs = [s - mean for s in slabs]
        spread = sum(jnp.sum(s * s, -1, keepdims=True) for s in slabs) * (1.0 / (4 * channels))
        scale = lax.rsqrt(spread + EPSILON)
        merged = None
        for p, s in enumerate(slabs):
            gain = gain_merge[...][None, p * channels : (p + 1) * channels]
            part = dot(
                (s * scale * gain).astype(BF16), merge_weight[p * channels : (p + 1) * channels, :]
            )
            merged = part if merged is None else merged + part
        merged = merged.astype(BF16)
        for w in range(group):
            n = first + w
            mbuf[n] = merged[w * patch : (w + 1) * patch].reshape(4, piece, wide)
            for a, b in ORDER:
                here, local, remote = owner_copy(n, a, b)
                pl.when(here)(local.start)
                pl.when(jnp.logical_not(here))(remote.start)
            for a, b in ORDER:
                home_copy(n, a, b).start()
        return carry

    lax.fori_loop(0, samples // group, fine, 0)

    bx, by = x - x % 2, y - y % 2
    me = (x % 2) * 2 + y % 2

    def result_copy(s, home):
        hx, hy = bx + home // 2, by + home % 2
        n = s * 4 + me
        local = pltpu.make_async_copy(obuf.at[s, home], coarse_out.at[n], o_recv)
        remote = pltpu.make_async_remote_copy(
            obuf.at[s, home], coarse_out.at[n], o_send.at[s, home], o_recv,
            device_id=(hx, hy), device_id_type=MESH,
        )
        return home == me, local, remote

    sides = (1 - x % 2, x % 2)

    def coarse(s, carry):
        pltpu.make_async_copy(cbuf.at[s], cbuf.at[s], c_recv.at[s]).wait()
        merged = jnp.concatenate(
            [cbuf[s, pl.ds(2 * part, 2)].reshape(2 * patch, wide) for part in sides], axis=0
        ).astype(F32)
        normed = normalize(merged, gain_coarse[...][None])
        q, k, v = (
            dot(normed, mixer_coarse[:, index * wide : (index + 1) * wide]).astype(BF16)
            for index in range(3)
        )
        for index, part in enumerate(sides):
            rows = slice(index * 2 * patch, (index + 1) * 2 * patch)
            out = merged[rows] + project(attention(q[rows], k, v), output_coarse)
            obuf[s, pl.ds(2 * part, 2)] = out.astype(BF16).reshape(2, patch, wide)
            for column in range(2):
                here, local, remote = result_copy(s, 2 * part + column)
                pl.when(here)(local.start)
                pl.when(jnp.logical_not(here))(remote.start)
        return carry

    for load in loads[8:]:
        load.wait()
    lax.fori_loop(0, samples // 4, coarse, 0)

    pltpu.make_async_copy(mhome, mhome, m_recv).wait()

    def settle(n, carry):
        for a, b in ORDER:
            if (a, b) != (1, 1):
                field_copy(n, a, b).wait_send()
            if (a, b) != (0, 0):
                home_copy(n, a, b).wait_send()
            here, _, remote = owner_copy(n, a, b)
            pl.when(jnp.logical_not(here))(remote.wait_send)
        return carry

    lax.fori_loop(0, samples, settle, 0)
    for s in range(samples // 4):
        for home in range(4):
            here, _, remote = result_copy(s, home)
            pl.when(jnp.logical_not(here))(remote.wait_send)
    pltpu.make_async_copy(coarse_out, coarse_out, o_recv).wait()


def natural_order(half, merged, coarse, merged_out, coarse_out):
    quarter = half // 2
    piece = quarter * quarter
    patch = 4 * piece
    row = lax.broadcasted_iota(jnp.int32, (patch, patch), 0)
    col = lax.broadcasted_iota(jnp.int32, (patch, patch), 1)
    down, across = row // half, row % half
    origin = (
        (down // quarter * 2 + across // quarter) * piece
        + (down % quarter) * quarter
        + across % quarter
    )
    order = (origin == col).astype(F32).astype(BF16)
    for n in range(merged.shape[0]):
        merged_out[n] = dot(order, merged[n]).astype(BF16)
        coarse_out[n] = dot(order, coarse[n]).astype(BF16)


def shards(nx, ny, fields, *weights):
    samples, side, _, channels = fields.shape
    half = side // 2
    wide = weights[7].shape[-1]
    piece = half * half // 4
    weights = [*weights[:5], weights[5].T, *weights[6:]]
    pieces = jax.ShapeDtypeStruct((samples, 4, piece, wide), BF16)
    shape = jax.ShapeDtypeStruct((samples, 4 * piece, wide), BF16)
    hbm = pl.BlockSpec(memory_space=pl.ANY)
    dma = pltpu.SemaphoreType.DMA
    merged, coarse = pl.pallas_call(
        functools.partial(kernel, nx, ny),
        out_shape=(pieces, shape),
        in_specs=[hbm] * (1 + len(weights)),
        out_specs=(hbm, hbm),
        scratch_shapes=[pltpu.VMEM(w.shape, w.dtype) for w in weights] + [
            pltpu.VMEM((samples, 4, half, half, channels), BF16),
            pltpu.VMEM((samples, 4, piece, wide), BF16),
            pltpu.VMEM((samples // 4, 4, 4, piece, wide), BF16),
            pltpu.VMEM((samples // 4, 4, 4 * piece, wide), BF16),
            pltpu.VMEM((3, channels, channels), BF16),
            pltpu.VMEM((side * side, side * side), BF16),
            dma((samples, 4)), dma((samples,)),
            dma((samples, 4)), dma,
            dma((samples, 4)), dma((samples // 4,)),
            dma((samples // 4, 4)), dma,
            dma((len(weights),)),
        ],
        compiler_params=pltpu.CompilerParams(
            collective_id=0, has_side_effects=True, vmem_limit_bytes=62 * 1024 * 1024
        ),
        name="encoder",
    )(fields.reshape(samples, side, 2, half, channels), *weights)
    steps = 2
    block = pl.BlockSpec((samples // steps, 4 * piece, wide), lambda step: (step, 0, 0))
    merged, coarse = pl.pallas_call(
        functools.partial(natural_order, half),
        grid=(steps,),
        out_shape=(shape, shape),
        in_specs=[block] * 2,
        out_specs=(block, block),
        name="natural_order",
    )(merged.reshape(shape.shape), coarse)
    return tuple(t.reshape(samples, half, half, wide) for t in (merged, coarse))


def solution(mesh):
    in_specs = (P(None, "gx", "gy", None),) + (P(),) * 11
    out_specs = (P(None, "gx", "gy", None), P(None, "gx", "gy", None))
    body = functools.partial(shards, mesh.shape["gx"], mesh.shape["gy"])
    return jax.shard_map(body, mesh=mesh, in_specs=in_specs, out_specs=out_specs, check_vma=False)
```

```python
import functools
import math

import jax
import jax.numpy as jnp
from jax import lax
from jax.experimental import pallas as pl
from jax.experimental.pallas import tpu as pltpu
from jax.sharding import PartitionSpec as P

HEAD = 32
LANES = 128
EPSILON = 1e-05
F32 = jnp.float32
BF16 = jnp.bfloat16
MESH = pl.DeviceIdType.MESH


def dot(a, b):
    return jnp.dot(a, b, preferred_element_type=F32)


def dot_nt(a, b):
    return lax.dot_general(a, b, (((1,), (1,)), ((), ())), preferred_element_type=F32)


def normalize(values, gain):
    center = values - jnp.mean(values, -1, keepdims=True)
    spread = jnp.mean(center * center, -1, keepdims=True)
    return (center * lax.rsqrt(spread + EPSILON) * gain).astype(BF16)


QUERY_SCALE = math.log2(math.e) / math.sqrt(HEAD)


def gelu(x):
    return 0.5 * x * (1.0 + lax.erf(x * (1.0 / math.sqrt(2.0))))


def attention(queries, keys, values):
    channels = queries.shape[-1]
    groups = []
    for low in range(0, channels, LANES):
        width = min(LANES, channels - low)
        q, k, v = (t[:, low : low + width] for t in (queries, keys, values))
        owner = lax.broadcasted_iota(jnp.int32, (1, width), 1) // HEAD
        context = None
        for head in range(width // HEAD):
            mine = owner == head
            scores = dot_nt(q * mine.astype(F32).astype(BF16), k)
            highest = jnp.max(scores, -1, keepdims=True)
            powers = jnp.exp2(scores - highest)
            total = jnp.sum(powers, -1, keepdims=True)
            part = dot(powers.astype(BF16), v) * (1.0 / total)
            context = part if context is None else jnp.where(mine, part, context)
        groups.append(context.astype(BF16))
    return groups


def project(groups, weight_ref):
    total = None
    for index, group in enumerate(groups):
        part = dot(group, weight_ref[index * LANES : index * LANES + group.shape[-1], :])
        total = part if total is None else total + part
    return total


def kernel(
    nx, ny,
    fields, *refs
):
    count = (len(refs) - 16) // 2
    weights_hbm, (mhome, coarse_out) = refs[:count], refs[count : count + 2]
    weights = refs[count + 2 : 2 * count + 2]
    (
        gain_window, mixer_fine, output_fine, gain_hidden, expand, contract,
        gain_merge, merge_weight, gain_coarse, mixer_coarse, output_coarse,
    ) = weights
    (
    fbuf, mbuf, cbuf, obuf, wsplit, perm_fine,
    f_send, f_recv, m_send, m_recv, c_send, c_recv, o_send, o_recv,
    w_recv,
    ) = refs[2 * count + 2 :]
    samples, _, half, _, channels = fbuf.shape
    side = 2 * half
    tokens = side * side
    quarter = half // 2
    piece = quarter * quarter
    patch = 4 * piece
    wide = mhome.shape[-1]
    x = lax.axis_index("gx")
    y = lax.axis_index("gy")

    def at(dx, dy):
        return (lax.rem(x + dx + nx, nx), lax.rem(y + dy + ny, ny))

    reach = [(dx, dy) for dx in (-1, 0, 1) for dy in (-1, 0, 1) if (dx, dy) != (0, 0)]
    barrier = pltpu.get_barrier_semaphore()
    for dx, dy in reach:
        pl.semaphore_signal(barrier, inc=1, device_id=at(dx, dy), device_id_type=MESH)
    loads = [
        pltpu.make_async_copy(source, target, w_recv.at[index])
        for index, (source, target) in enumerate(zip(weights_hbm, weights))
    ]
    for load in loads:
        load.start()
    def field_copy(n, a, b):
        slot = (1 - a) * 2 + (1 - b)
        source = fields.at[n, pl.ds(a * half, half), b]
        target = fbuf.at[n, slot]
        if a == 1 and b == 1:
            return pltpu.make_async_copy(source, target, f_recv.at[n])
        return pltpu.make_async_remote_copy(
            source, target, f_send.at[n, slot], f_recv.at[n],
            device_id=at(a - 1, b - 1), device_id_type=MESH,
        )

    ORDER = ((0, 0), (0, 1), (1, 0), (1, 1))

    pl.semaphore_wait(barrier, len(reach))

    def start_fields(n, carry):
        for a, b in ORDER:
            field_copy(n, a, b).start()
        return carry

    ahead = min(4, samples)
    lax.fori_loop(0, ahead, start_fields, 0)

    for load in loads[:8]:
        load.wait()
    for index in range(3):
        wsplit[index] = mixer_fine[:, index * channels : (index + 1) * channels]
    row = lax.broadcasted_iota(jnp.int32, (tokens, tokens), 0)
    col = lax.broadcasted_iota(jnp.int32, (tokens, tokens), 1)
    parity, rest = row // patch, row % patch
    quadrant, within = rest // piece, rest % piece
    origin = (
        quadrant * (half * half)
        + (2 * (within // quarter) + parity % 2) * half
        + 2 * (within % quarter)
        + parity // 2
    )
    perm_fine[...] = (origin == col).astype(F32).astype(BF16)
    def home_copy(n, a, b):
        source = mbuf.at[n, a * 2 + b]
        target = mhome.at[n, (1 - a) * 2 + (1 - b)]
        if a == 0 and b == 0:
            return pltpu.make_async_copy(source, target, m_recv)
        return pltpu.make_async_remote_copy(
            source, target, m_send.at[n, a * 2 + b], m_recv,
            device_id=at(a, b), device_id_type=MESH,
        )

    def owner_copy(n, a, b):
        hx, hy = at(a, b)
        member = n % 4
        ox = hx - hx % 2 + member // 2
        oy = hy - hy % 2 + member % 2
        source = mbuf.at[n, a * 2 + b]
        target = cbuf.at[n // 4, (hx % 2) * 2 + hy % 2, (1 - a) * 2 + (1 - b)]
        here = jnp.logical_and(ox == x, oy == y)
        local = pltpu.make_async_copy(source, target, c_recv.at[n // 4])
        remote = pltpu.make_async_remote_copy(
            source, target, c_send.at[n, a * 2 + b], c_recv.at[n // 4],
            device_id=(ox, oy), device_id_type=MESH,
        )
        return here, local, remote

    group = 2

    def fine(step, carry):
        first = step * group

        for w in range(group):
            @pl.when(first + w + ahead < samples)
            def _():
                start_fields(first + w + ahead, 0)

        values = []
        for w in range(group):
            n = first + w
            pltpu.make_async_copy(fbuf.at[n], fbuf.at[n], f_recv.at[n]).wait()
            window = fbuf[n].astype(F32).reshape(tokens, channels).astype(BF16)
            values.append(dot(perm_fine[...], window))
        value = jnp.concatenate(values, axis=0)
        normed = normalize(value, gain_window[...][None])
        q = (dot(normed, wsplit[0]) * QUERY_SCALE).astype(BF16)
        k, v = (dot(normed, wsplit[index]).astype(BF16) for index in (1, 2))
        parts = [
            attention(*(t[w * tokens : (w + 1) * tokens] for t in (q, k, v)))
            for w in range(group)
        ]
        context = [jnp.concatenate(c, axis=0) for c in zip(*parts)]
        attended = (value + project(context, output_fine)).astype(BF16).astype(F32)
        normed = normalize(attended, gain_hidden[...][None])
        hidden = gelu(dot(normed, expand[...])).astype(BF16)
        refined = (attended + dot_nt(hidden, contract[...])).astype(BF16).astype(F32)
        slabs = [
            jnp.concatenate(
                [refined[w * tokens + p * patch : w * tokens + (p + 1) * patch] for w in range(group)],
                axis=0,
            )
            for p in range(4)
        ]
        mean = sum(jnp.sum(s, -1, keepdims=True) for s in slabs) * (1.0 / (4 * channels))
        slabs = [s - mean for s in slabs]
        spread = sum(jnp.sum(s * s, -1, keepdims=True) for s in slabs) * (1.0 / (4 * channels))
        scale = lax.rsqrt(spread + EPSILON)
        merged = None
        for p, s in enumerate(slabs):
            gain = gain_merge[...][None, p * channels : (p + 1) * channels]
            part = dot(
                (s * scale * gain).astype(BF16), merge_weight[p * channels : (p + 1) * channels, :]
            )
            merged = part if merged is None else merged + part
        merged = merged.astype(BF16)
        for w in range(group):
            n = first + w
            mbuf[n] = merged[w * patch : (w + 1) * patch].reshape(4, piece, wide)
            for a, b in ORDER:
                here, local, remote = owner_copy(n, a, b)
                pl.when(here)(local.start)
                pl.when(jnp.logical_not(here))(remote.start)
            for a, b in ORDER:
                home_copy(n, a, b).start()
        return carry

    lax.fori_loop(0, samples // group, fine, 0)

    bx, by = x - x % 2, y - y % 2
    me = (x % 2) * 2 + y % 2

    def result_copy(s, home):
        hx, hy = bx + home // 2, by + home % 2
        n = s * 4 + me
        local = pltpu.make_async_copy(obuf.at[s, home], coarse_out.at[n], o_recv)
        remote = pltpu.make_async_remote_copy(
            obuf.at[s, home], coarse_out.at[n], o_send.at[s, home], o_recv,
            device_id=(hx, hy), device_id_type=MESH,
        )
        return home == me, local, remote

    sides = (1 - x % 2, x % 2)

    def coarse(s, carry):
        pltpu.make_async_copy(cbuf.at[s], cbuf.at[s], c_recv.at[s]).wait()
        merged = jnp.concatenate(
            [cbuf[s, pl.ds(2 * part, 2)].reshape(2 * patch, wide) for part in sides], axis=0
        ).astype(F32)
        normed = normalize(merged, gain_coarse[...][None])
        q = (dot(normed, mixer_coarse[:, :wide]) * QUERY_SCALE).astype(BF16)
        k, v = (
            dot(normed, mixer_coarse[:, index * wide : (index + 1) * wide]).astype(BF16)
            for index in (1, 2)
        )
        for index, part in enumerate(sides):
            rows = slice(index * 2 * patch, (index + 1) * 2 * patch)
            out = merged[rows] + project(attention(q[rows], k, v), output_coarse)
            obuf[s, pl.ds(2 * part, 2)] = out.astype(BF16).reshape(2, patch, wide)
            for column in range(2):
                here, local, remote = result_copy(s, 2 * part + column)
                pl.when(here)(local.start)
                pl.when(jnp.logical_not(here))(remote.start)
        return carry

    for load in loads[8:]:
        load.wait()
    lax.fori_loop(0, samples // 4, coarse, 0)

    pltpu.make_async_copy(mhome, mhome, m_recv).wait()

    def settle(n, carry):
        for a, b in ORDER:
            if (a, b) != (1, 1):
                field_copy(n, a, b).wait_send()
            if (a, b) != (0, 0):
                home_copy(n, a, b).wait_send()
            here, _, remote = owner_copy(n, a, b)
            pl.when(jnp.logical_not(here))(remote.wait_send)
        return carry

    lax.fori_loop(0, samples, settle, 0)
    for s in range(samples // 4):
        for home in range(4):
            here, _, remote = result_copy(s, home)
            pl.when(jnp.logical_not(here))(remote.wait_send)
    pltpu.make_async_copy(coarse_out, coarse_out, o_recv).wait()


def natural_order(half, merged, coarse, merged_out, coarse_out):
    quarter = half // 2
    piece = quarter * quarter
    patch = 4 * piece
    row = lax.broadcasted_iota(jnp.int32, (patch, patch), 0)
    col = lax.broadcasted_iota(jnp.int32, (patch, patch), 1)
    down, across = row // half, row % half
    origin = (
        (down // quarter * 2 + across // quarter) * piece
        + (down % quarter) * quarter
        + across % quarter
    )
    order = (origin == col).astype(F32).astype(BF16)
    for n in range(merged.shape[0]):
        merged_out[n] = dot(order, merged[n]).astype(BF16)
        coarse_out[n] = dot(order, coarse[n]).astype(BF16)


def shards(nx, ny, fields, *weights):
    samples, side, _, channels = fields.shape
    half = side // 2
    wide = weights[7].shape[-1]
    piece = half * half // 4
    weights = [*weights[:5], weights[5].T, *weights[6:]]
    pieces = jax.ShapeDtypeStruct((samples, 4, piece, wide), BF16)
    shape = jax.ShapeDtypeStruct((samples, 4 * piece, wide), BF16)
    hbm = pl.BlockSpec(memory_space=pl.ANY)
    dma = pltpu.SemaphoreType.DMA
    merged, coarse = pl.pallas_call(
        functools.partial(kernel, nx, ny),
        out_shape=(pieces, shape),
        in_specs=[hbm] * (1 + len(weights)),
        out_specs=(hbm, hbm),
        scratch_shapes=[pltpu.VMEM(w.shape, w.dtype) for w in weights] + [
            pltpu.VMEM((samples, 4, half, half, channels), BF16),
            pltpu.VMEM((samples, 4, piece, wide), BF16),
            pltpu.VMEM((samples // 4, 4, 4, piece, wide), BF16),
            pltpu.VMEM((samples // 4, 4, 4 * piece, wide), BF16),
            pltpu.VMEM((3, channels, channels), BF16),
            pltpu.VMEM((side * side, side * side), BF16),
            dma((samples, 4)), dma((samples,)),
            dma((samples, 4)), dma,
            dma((samples, 4)), dma((samples // 4,)),
            dma((samples // 4, 4)), dma,
            dma((len(weights),)),
        ],
        compiler_params=pltpu.CompilerParams(
            collective_id=0, has_side_effects=True, vmem_limit_bytes=62 * 1024 * 1024
        ),
        name="encoder",
    )(fields.reshape(samples, side, 2, half, channels), *weights)
    steps = 2
    block = pl.BlockSpec((samples // steps, 4 * piece, wide), lambda step: (step, 0, 0))
    merged, coarse = pl.pallas_call(
        functools.partial(natural_order, half),
        grid=(steps,),
        out_shape=(shape, shape),
        in_specs=[block] * 2,
        out_specs=(block, block),
        name="natural_order",
    )(merged.reshape(shape.shape), coarse)
    return tuple(t.reshape(samples, half, half, wide) for t in (merged, coarse))


def solution(mesh):
    in_specs = (P(None, "gx", "gy", None),) + (P(),) * 11
    out_specs = (P(None, "gx", "gy", None), P(None, "gx", "gy", None))
    body = functools.partial(shards, mesh.shape["gx"], mesh.shape["gy"])
    return jax.shard_map(body, mesh=mesh, in_specs=in_specs, out_specs=out_specs, check_vma=False)
```
